32 devices in a mesh: rec: 4 (over y, core), tm: 8 (over z, x).
Axes of the slice: x: 2, y: 2, z: 4, core: 2. Of those that a mesh axis runs over, the one named last changes fastest.
Arguments:
- wave: float32 [64, 262144], P('rec', 'tm'), parts along dimension 0, may hold values from -6 to 6
- target_mod: float32 [6144, 256], P(('rec', 'tm')), parts along dimension 0, may hold values from 0 to 0.5
- lengths: int32 [64], P('rec'), parts along dimension 0, may hold values from 256 to 1024, as said below
Outputs:
- grad_wave: float32 [64, 262144], P('rec', 'tm'), parts along dimension 0
- loss: float32 [64], P('rec'), parts along dimension 0
The draws below stay inside these ranges and needn't reach their ends.
There are 4 independent parts, one for each index of `rec`. The reference program is written for one: setup_inputs(seed, part) draws one part's arguments, and reference() takes and returns one part's arrays. A program takes and returns all parts, laid end to end along the dimension named above; each array names one. Nothing has to cross between parts.
Inputs may be any that keep to these rules, and one draw needn't show every extreme that they name: lengths[r] counts frames from the start of recording r; in every part some recording has all 1024 frames valid.
All inputs are finite; a program needn't handle non-finite values.
Results may differ from the reference program's by a relative error of at most 0.00027.
Values sent between devices are 32-bit elements; how exact they have to be, the bound alone decides.
No kernel may reach another device: no remote copies, remote signals or barrier semaphores. Data moves between devices by JAX's collectives and lax.ppermute only.
A program may use at most 128 MiB of HBM per device.

```python
import math
import jax
import jax.numpy as jnp
from jax import lax

RECORDS = 16
FFT = 512
BANDS = 96
FRAMES = 1024
K = 256
ROWS = 1536
SAMPLES = 262144


def draw_lengths(key, part):
    first_key, second_key = jax.random.split(jax.random.fold_in(key, 17))
    values = jax.random.randint(first_key, (RECORDS,), FRAMES // 4, FRAMES + 1)
    chosen = jax.random.randint(second_key, (), 0, RECORDS)
    return jnp.where(jnp.arange(RECORDS) == chosen, FRAMES, values).astype(jnp.int32)


def level_of(rng, shape, cuts, low, largest):
    gain, own = 1.0, jax.random.fold_in(rng, 6)
    for position, shards_of in cuts:
        steps = jnp.exp(jax.random.uniform(jax.random.fold_in(own, position), (shards_of,), jnp.float32, low / len(cuts), largest / len(cuts)))
        gain = gain * jnp.repeat(steps, shape[position] // shards_of).reshape([-1 if axis == position else 1 for axis in range(len(shape))])
    return gain


def bell_draw(stream_key, extent, deviation, most, pieces=(), kind=jnp.bfloat16):
    drawn = jax.random.normal(stream_key, extent, jnp.float32) * deviation
    if len(pieces) > 0:
        drawn = level_of(stream_key, extent, pieces, -0.22, 0.18) * drawn
    return jnp.clip(drawn, min=-most, max=most).astype(kind)


def setup_inputs(seed: int = 0, part: int = 0) -> dict:
    key_of = jax.random.split(jax.random.key(seed), 4)
    part_splits = jax.random.split(jax.random.fold_in(key_of[3], part), 4)
    return {
        "wave": bell_draw(part_splits[0], (RECORDS, SAMPLES), 1.0, 6.0, ((1, 8),), jnp.float32),
        "target_mod": jnp.clip(0.5 * jax.random.uniform(part_splits[1], (ROWS, K), jnp.float32) ** level_of(part_splits[1], (ROWS, K), ((0, 8),), -0.2, 0.2), 0.0, 0.5),
        "lengths": draw_lengths(jax.random.fold_in(jax.random.fold_in(key_of[3], part), 71), part),
    }


HIGH = lax.Precision.HIGHEST
rate_hz = 16000.0

def a_weight(freq):
    square = freq * freq
    upper = 12194.0 ** 2 * square * square
    lower = (square + 20.6 ** 2) * jnp.sqrt((square + 107.7 ** 2) * (square + 737.9 ** 2)) * (square + 12194.0 ** 2)
    return upper / lower

def bark_scale(freq):
    return 13.0 * jnp.arctan(0.00076 * freq) + 3.5 * jnp.arctan((freq / 7500.0) ** 2)

def band_table(bins, bands):
    freq = jnp.arange(bins, dtype=jnp.float32) * (rate_hz / (2.0 * bins))
    height = bark_scale(freq)
    top_bark = bark_scale(jnp.asarray(rate_hz / 2.0, jnp.float32))
    centres = (jnp.arange(bands, dtype=jnp.float32) + 0.5) * (top_bark / bands)
    spread = jnp.maximum(0.5, 2.0 * top_bark / bands)
    shape = jnp.maximum(0.0, 1.0 - jnp.abs(height[:, None] - centres[None, :]) / spread)
    weight = 0.1 + a_weight(freq) / a_weight(jnp.asarray(1000.0, jnp.float32))
    return shape * weight[:, None] / jnp.maximum(lax.optimization_barrier(jnp.sum(shape, axis=0)), 1.0)[None, :]

def spectral_table(size):
    bins = size // 2
    index = jnp.arange(size, dtype=jnp.int32)[:, None] * jnp.arange(bins, dtype=jnp.int32)[None, :] % size
    angle = index.astype(jnp.float32) * (2.0 * math.pi / size)
    return jnp.concatenate([jnp.cos(angle), -jnp.sin(angle)], axis=1) * (1.0 / math.sqrt(size))

def hann_window(size):
    return 0.5 - 0.5 * jnp.cos(jnp.arange(size, dtype=jnp.float32) * (2.0 * math.pi / size))

def modulation_table(times, count, length):
    index = times[:, None] * jnp.arange(1, count + 1, dtype=jnp.int32)[None, :] % length
    angle = index.astype(jnp.float32) * (2.0 * math.pi / length)
    return jnp.concatenate([jnp.cos(angle), -jnp.sin(angle)], axis=1) * (1.0 / math.sqrt(length))

def reference(wave, target_mod, lengths):
    records = wave.shape[0]
    half = FFT // 2
    window = hann_window(FFT)
    spectral = spectral_table(FFT)
    filters = band_table(half, BANDS)
    padded = jnp.concatenate([wave, jnp.zeros((records, half), jnp.float32)], axis=1)
    blocks = padded.reshape(records, FRAMES + 1, half)
    frames = jnp.concatenate([blocks[:, :-1], blocks[:, 1:]], axis=2) * window
    spectrum = jnp.einsum('rfn,nk->rfk', frames, spectral, precision=HIGH)
    real_stft = spectrum[..., :half]
    imag_stft = spectrum[..., half:]
    power = real_stft * real_stft + imag_stft * imag_stft
    energy = jnp.einsum('rfk,kb->rbf', power, filters, precision=HIGH)
    envelope = (energy + 0.05) ** 0.3
    times = jnp.arange(FRAMES, dtype=jnp.int32)
    valid = (times[None, :] < lengths[:, None]).astype(jnp.float32)
    masked = envelope * valid[:, None, :]
    counts = lengths.astype(jnp.float32) * BANDS
    loudness = lax.optimization_barrier(jnp.sum(masked, axis=(1, 2))) / counts + 1e-05
    normed = masked / loudness[:, None, None]
    table = modulation_table(times, K, FRAMES)
    spectra = jnp.dot(normed.reshape(records * BANDS, FRAMES), table, precision=HIGH, preferred_element_type=jnp.float32)
    real_mod = spectra[:, :K]
    imag_mod = spectra[:, K:]
    mod_power = real_mod * real_mod + imag_mod * imag_mod
    mismatch = jnp.log1p(mod_power) - target_mod
    loss = 0.5 * lax.optimization_barrier(jnp.sum((mismatch * mismatch).reshape(records, -1), axis=1))
    factor = 2.0 * mismatch / (1.0 + mod_power)
    grad_real = factor * real_mod
    grad_imag = factor * imag_mod
    inner = lax.optimization_barrier(jnp.sum((grad_real * real_mod + grad_imag * imag_mod).reshape(records, -1), axis=1))
    grad_spectra = jnp.concatenate([grad_real, grad_imag], axis=1)
    grad_normed = lax.dot_general(grad_spectra, table, (((1,), (1,)), ((), ())), precision=HIGH, preferred_element_type=jnp.float32)
    grad_normed = grad_normed.reshape(records, BANDS, FRAMES)
    grad_env = (grad_normed - (inner / counts)[:, None, None]) / loudness[:, None, None] * valid[:, None, :]
    grad_energy = 0.3 * (energy + 0.05) ** (-0.7) * grad_env
    grad_power = jnp.einsum('rbf,kb->rfk', grad_energy, filters, precision=HIGH)
    grad_spectrum = jnp.concatenate([2.0 * real_stft * grad_power, 2.0 * imag_stft * grad_power], axis=2)
    grad_frames = jnp.einsum('rfk,nk->rfn', grad_spectrum, spectral, precision=HIGH) * window
    leading = grad_frames[..., :half]
    trailing = grad_frames[..., half:]
    spare = jnp.zeros((records, 1, half), jnp.float32)
    summed = jnp.concatenate([leading, spare], axis=1) + jnp.concatenate([spare, trailing], axis=1)
    grad_wave = summed[:, :FRAMES].reshape(records, FRAMES * half)
    return (grad_wave, loss)
```

```python
import functools
import math

import jax
import jax.numpy as jnp
import numpy as np
from jax import lax
from jax.experimental import pallas as pl
from jax.experimental.pallas import tpu as pltpu
from jax.sharding import PartitionSpec as P

FFT = 512
BANDS = 96


HIGH = lax.Precision.HIGHEST
rate_hz = 16000.0


def from_behind(array, axis, by):
    count = lax.axis_size(axis)
    pairs = [(i, i + by) for i in range(count) if 0 <= i + by < count]
    return lax.ppermute(array, axis, pairs)


def a_weight(freq):
    square = freq * freq
    upper = 12194.0**2 * square * square
    lower = (
        (square + 20.6**2)
        * jnp.sqrt((square + 107.7**2) * (square + 737.9**2))
        * (square + 12194.0**2)
    )
    return upper / lower


def bark_scale(freq):
    return 13.0 * jnp.arctan(0.00076 * freq) + 3.5 * jnp.arctan((freq / 7500.0) ** 2)


def band_table(bins, bands):
    freq = jnp.arange(bins, dtype=jnp.float32) * (rate_hz / (2.0 * bins))
    height = bark_scale(freq)
    top_bark = bark_scale(jnp.asarray(rate_hz / 2.0, jnp.float32))
    centres = (jnp.arange(bands, dtype=jnp.float32) + 0.5) * (top_bark / bands)
    spread = jnp.maximum(0.5, 2.0 * top_bark / bands)
    shape = jnp.maximum(0.0, 1.0 - jnp.abs(height[:, None] - centres[None, :]) / spread)
    weight = 0.1 + a_weight(freq) / a_weight(jnp.asarray(1000.0, jnp.float32))
    return shape * weight[:, None] / jnp.maximum(jnp.sum(shape, axis=0), 1.0)[None, :]


def spectral_table(size):
    bins = size // 2
    index = (
        jnp.arange(size, dtype=jnp.int32)[:, None]
        * jnp.arange(bins, dtype=jnp.int32)[None, :]
        % size
    )
    angle = index.astype(jnp.float32) * (2.0 * math.pi / size)
    return jnp.concatenate([jnp.cos(angle), -jnp.sin(angle)], axis=1) * (1.0 / math.sqrt(size))


def hann_window(size):
    return 0.5 - 0.5 * jnp.cos(jnp.arange(size, dtype=jnp.float32) * (2.0 * math.pi / size))


def modulation_table(times, count, length):
    index = times[:, None] * jnp.arange(1, count + 1, dtype=jnp.int32)[None, :] % length
    angle = index.astype(jnp.float32) * (2.0 * math.pi / length)
    return jnp.concatenate([jnp.cos(angle), -jnp.sin(angle)], axis=1) * (1.0 / math.sqrt(length))


def general_body(wave, target_mod, lengths):
    records = wave.shape[0]
    half = FFT // 2
    frames_dev = wave.shape[1] // half
    devices = lax.axis_size("tm")
    position = lax.axis_index("tm")
    rows_dev = target_mod.shape[0]
    count = target_mod.shape[1]
    frames_all = frames_dev * devices
    window = hann_window(FFT)
    spectral = spectral_table(FFT)
    filters = band_table(half, BANDS)
    blocks = wave.reshape(records, frames_dev, half)
    following = from_behind(blocks[:, 0, :], "tm", -1)
    extended = jnp.concatenate([blocks, following[:, None, :]], axis=1)
    frames = jnp.concatenate([extended[:, :-1], extended[:, 1:]], axis=2) * window
    spectrum = jnp.einsum("rfn,nk->rfk", frames, spectral, precision=HIGH)
    real_stft = spectrum[..., :half]
    imag_stft = spectrum[..., half:]
    power = real_stft * real_stft + imag_stft * imag_stft
    energy = jnp.einsum("rfk,kb->rbf", power, filters, precision=HIGH)
    envelope = (energy + 0.05) ** 0.3
    times = position * frames_dev + jnp.arange(frames_dev, dtype=jnp.int32)
    valid = (times[None, :] < lengths[:, None]).astype(jnp.float32)
    masked = envelope * valid[:, None, :]
    counts = lengths.astype(jnp.float32) * BANDS
    partial_value = jnp.sum(masked, axis=(1, 2))
    row_ids = position * rows_dev + jnp.arange(rows_dev, dtype=jnp.int32)
    owner = row_ids // BANDS
    picker = (owner[:, None] == jnp.arange(records, dtype=jnp.int32)[None, :]).astype(jnp.float32)
    flat = masked.reshape(records * BANDS, frames_dev)
    full_table = modulation_table(jnp.arange(frames_all, dtype=jnp.int32), count, frames_all)
    stacked = flat.reshape(devices, rows_dev, frames_dev)
    spectra = jnp.dot(
        lax.all_to_all(stacked, "tm", split_axis=0, concat_axis=2, tiled=True)[0],
        full_table,
        precision=HIGH,
        preferred_element_type=jnp.float32,
    )
    loudness = lax.psum(partial_value, "tm") / counts + 1e-05
    spectra = spectra / jnp.dot(picker, loudness, precision=HIGH)[:, None]
    real_mod = spectra[:, :count]
    imag_mod = spectra[:, count:]
    mod_power = real_mod * real_mod + imag_mod * imag_mod
    mismatch = jnp.log1p(mod_power) - target_mod
    factor = 2.0 * mismatch / (1.0 + mod_power)
    grad_real = factor * real_mod
    grad_imag = factor * imag_mod
    loss_part = jnp.dot(0.5 * jnp.sum(mismatch * mismatch, axis=1), picker, precision=HIGH)
    inner_part = jnp.dot(
        jnp.sum(grad_real * real_mod + grad_imag * imag_mod, axis=1), picker, precision=HIGH
    )
    loss, inner = lax.psum((loss_part, inner_part), "tm")
    grad_spectra = jnp.concatenate([grad_real, grad_imag], axis=1)
    grad_bands = lax.dot_general(
        grad_spectra,
        full_table,
        (((1,), (1,)), ((), ())),
        precision=HIGH,
        preferred_element_type=jnp.float32,
    )
    grad_rows = lax.all_to_all(grad_bands, "tm", split_axis=1, concat_axis=0, tiled=True)
    grad_normed = grad_rows.reshape(records, BANDS, frames_dev)
    grad_env = (
        (grad_normed - (inner / counts)[:, None, None])
        / loudness[:, None, None]
        * valid[:, None, :]
    )
    grad_energy = 0.3 * (energy + 0.05) ** (-0.7) * grad_env
    grad_power = jnp.einsum("rbf,kb->rfk", grad_energy, filters, precision=HIGH)
    grad_spectrum = jnp.concatenate(
        [2.0 * real_stft * grad_power, 2.0 * imag_stft * grad_power], axis=2
    )
    grad_frames = jnp.einsum("rfk,nk->rfn", grad_spectrum, spectral, precision=HIGH) * window
    leading = grad_frames[..., :half]
    trailing = grad_frames[..., half:]
    arrived = from_behind(trailing[:, -1, :], "tm", 1)
    moved = jnp.concatenate([arrived[:, None, :], trailing[:, :-1]], axis=1)
    grad_wave = (leading + moved).reshape(records, frames_dev * half)
    return (grad_wave, loss)


F32, BF16 = jnp.float32, jnp.bfloat16
CHUNK, BACK_CHUNK = 32, 64


def split_table(table):
    table = np.asarray(table, np.float32)
    high = table.astype(BF16)
    low = (table - high.astype(np.float32)).astype(BF16)
    return high, low


def paired(table):
    return np.stack(split_table(table))


def host_window(size):
    return (0.5 - 0.5 * np.cos(np.arange(size) * (2.0 * np.pi / size))).astype(np.float32)


def host_filters(bins, bands):
    freq = np.arange(bins) * (rate_hz / (2.0 * bins))

    def bark(f):
        return 13.0 * np.arctan(0.00076 * f) + 3.5 * np.arctan((f / 7500.0) ** 2)

    def weight_of(f):
        square = f * f
        upper = 12194.0**2 * square * square
        lower = (
            (square + 20.6**2)
            * np.sqrt((square + 107.7**2) * (square + 737.9**2))
            * (square + 12194.0**2)
        )
        return upper / lower

    height, top = bark(freq), bark(rate_hz / 2.0)
    centres = (np.arange(bands) + 0.5) * (top / bands)
    spread = max(0.5, 2.0 * top / bands)
    shape = np.maximum(0.0, 1.0 - np.abs(height[:, None] - centres[None, :]) / spread)
    weight = 0.1 + weight_of(freq) / weight_of(1000.0)
    return shape * weight[:, None] / np.maximum(shape.sum(axis=0), 1.0)[None, :]


def host_halves(size):
    half, quarter = size // 2, size // 4
    n, m = np.arange(half)[:, None], np.arange(quarter)[None, :]
    tables = []
    for odd in range(2):
        angle = (n * (2 * m + odd) % size) * (2.0 * np.pi / size)
        tables.append(np.concatenate([np.cos(angle), -np.sin(angle)], axis=1) / np.sqrt(size))
    return tables


def host_modulation(length, count):
    tables = []
    for first in (2, 1):
        index = np.arange(length // 2)[:, None] * np.arange(first, count + 1, 2)[None, :] % length
        angle = index * (2.0 * np.pi / length)
        tables.append(np.concatenate([np.cos(angle), -np.sin(angle)], axis=1) / np.sqrt(length))
    return tables


def host_order(count):
    order = np.concatenate([np.arange(1, count, 2), np.arange(0, count, 2)])
    return (np.arange(count)[:, None] == order[None, :]).astype(BF16)


def parts(value):
    high = value.astype(BF16)
    return high, (value - high.astype(F32)).astype(BF16)


NN, NT, TN = (((1,), (0,)), ((), ())), (((1,), (1,)), ((), ())), (((0,), (0,)), ((), ()))


def product(value, table, dims, axis=1, table_axis=0):
    high, low = parts(value)
    left = jnp.concatenate([high, low, high], axis=axis)
    right = jnp.concatenate([table[0], table[0], table[1]], axis=table_axis)
    return lax.dot_general(left, right, dims, preferred_element_type=F32)


def swapped(position, s, per, j):
    return lax.bitwise_xor(position, s) * per + j


def spectrum(left, right, even, odd):
    return product(left + right, even, NN), product(left - right, odd, NN)


def power_of(bins):
    quarter = bins.shape[1] // 2
    return bins[:, :quarter] * bins[:, :quarter] + bins[:, quarter:] * bins[:, quarter:]


def band_energy(power, filters):
    high, low = parts(power)
    right = jnp.concatenate([high, low, high], axis=1)
    left = jnp.concatenate([filters[0], filters[0], filters[1]], axis=1)
    return lax.dot_general(left, right, NT, preferred_element_type=F32) + 0.05


def compress(base):
    envelope = jnp.exp(0.3 * jnp.log(base))
    return envelope, 0.6 * envelope / base


def analyse(devices, per, me_ref, len_ref, x_ref, next_ref, win_ref, even_ref, odd_ref, filt_ref,
            stft_ref, env_ref, ratio_ref, *powers):
    records, half = next_ref.shape
    frames = powers[0].shape[0] // records
    step, last = pl.program_id(0), pl.num_programs(0) - 1
    w0, w1 = win_ref[0:1, :half], win_ref[0:1, half:]
    left, right = [], []
    for t in range(CHUNK):
        left.append(x_ref[:, half * t : half * (t + 1)] * w0)
        after = x_ref[:, half * (t + 1) : half * (t + 2)] if t + 1 < CHUNK else next_ref[...]
        right.append(after * w1)
    size = CHUNK * records
    rows = pl.ds(pl.multiple_of(step * size, size), size)
    left, right = jnp.concatenate(left, axis=0), jnp.concatenate(right, axis=0)
    for which, bins in enumerate(spectrum(left, right, even_ref, odd_ref)):
        stft_ref[:, :, which * half : (which + 1) * half] = bins.reshape(CHUNK, records, half)
        powers[which][rows, :] = power_of(bins)

    @pl.when(step == last)
    def _():
        me = me_ref[0]
        times = me * frames + lax.broadcasted_iota(jnp.int32, (BANDS, frames), 1)
        for s in range(devices):
            for j in range(per):
                record = swapped(me, s, per, j)
                at = pl.ds(record, frames, stride=records)
                mine = jnp.concatenate([power[at, :] for power in powers], axis=1)
                envelope, ratio = compress(band_energy(mine, filt_ref))
                valid = times < len_ref[record]
                env_ref[s, j] = jnp.where(valid, envelope, 0.0)
                ratio_ref[s, j] = jnp.where(valid, ratio, 0.0)


def finish(devices, per, me_ref, len_ref, last_ref, halo_ref, win_ref, even_ref, odd_ref, filt_ref,
           env_ref, ratio_ref, stft_ref, out_ratio_ref, send_ref, *rest):
    out_refs, power = rest[:devices], rest[devices]
    half = halo_ref.shape[1]
    frames = env_ref.shape[3]
    me = me_ref[0]
    w0, w1 = win_ref[0:1, :half], win_ref[0:1, half:]
    bins = spectrum(last_ref[...] * w0, halo_ref[...] * w1, even_ref, odd_ref)
    stft_ref[...] = jnp.concatenate(bins, axis=1)
    send_ref[...] = last_ref[...]
    power[...] = jnp.concatenate([power_of(b) for b in bins], axis=1)
    ordered = [power[pl.ds(swapped(me, s, per, j), 1), :] for s in range(devices) for j in range(per)]
    envelope, ratio = compress(band_energy(jnp.concatenate(ordered, axis=0), filt_ref))
    newest = lax.broadcasted_iota(jnp.int32, (BANDS, frames), 1) == frames - 1
    at = me * frames + frames - 1
    for s in range(devices):
        for j in range(per):
            k = s * per + j
            valid = at < len_ref[swapped(me, s, per, j)]
            here = jnp.where(valid, envelope[:, k : k + 1], 0.0)
            out_refs[s][j * BANDS : (j + 1) * BANDS, :] = jnp.where(newest, here, env_ref[s, j])
            here = jnp.where(valid, ratio[:, k : k + 1], 0.0)
            out_ratio_ref[s, j] = jnp.where(newest, here, ratio_ref[s, j])


def modulate(devices, per, me_ref, len_ref, *rest):
    env_refs, rest = rest[:devices], rest[devices:]
    target_ref, order_ref, even_ref, odd_ref, edge_ref = rest[:5]
    out_refs, (held_ref, edge_rows) = rest[5 : 5 + devices], rest[5 + devices :]
    me = me_ref[0]
    rows, frames = env_refs[0].shape
    count = target_ref.shape[1]
    middle = count // 2
    half = held_ref.shape[1] // 2
    for s in range(devices):
        at = pl.ds(pl.multiple_of(lax.bitwise_xor(me, s) * frames, frames), frames)
        held_ref[:, at] = env_refs[s][...]
    early, late = held_ref[:, :half], held_ref[:, half:]
    total = early + late
    spectra = product(total, even_ref, NN), product(early - late, odd_ref, NN)
    target = target_ref[...]
    high, low = parts(target)
    least = (target - high.astype(F32) - low.astype(F32)).astype(BF16)
    order = order_ref[...]
    target = lax.dot_general(
        jnp.concatenate([high, low, least], axis=1),
        jnp.concatenate([order, order, order], axis=0),
        NN,
        preferred_element_type=F32,
    )
    grads, shifts = [[], []], []
    for j in range(per):
        at = slice(j * BANDS, (j + 1) * BANDS)
        counts = len_ref[me * per + j].astype(F32) * BANDS
        loudness = jnp.sum(total[at], axis=(0, 1), keepdims=True) / counts + 1e-05
        loss, inner = jnp.zeros((1, 1), F32), jnp.zeros((1, 1), F32)
        for which in range(2):
            mine = spectra[which][at] / loudness
            real, imag = mine[:, :middle], mine[:, middle:]
            mod_power = real * real + imag * imag
            mismatch = jnp.log1p(mod_power) - target[at, which * middle : (which + 1) * middle]
            factor = 2.0 * mismatch / (1.0 + mod_power)
            loss += 0.5 * jnp.sum(mismatch * mismatch, axis=(0, 1), keepdims=True)
            inner += jnp.sum(factor * mod_power, axis=(0, 1), keepdims=True)
            factor = factor / loudness
            grads[which].append(jnp.concatenate([factor * real, factor * imag], axis=1))
        shift = inner / counts / loudness
        shifts.append(jnp.broadcast_to(shift, (BANDS, 1)))
        edge = jnp.zeros((edge_ref.shape[2], BANDS), F32)
        for which in range(2):
            high, low = parts(grads[which][j])
            left = jnp.concatenate([edge_ref[which, 0], edge_ref[which, 0], edge_ref[which, 1]], axis=1)
            right = jnp.concatenate([high, low, high], axis=1)
            edge += lax.dot_general(left, right, NT, preferred_element_type=F32)
        spare = jnp.broadcast_to(loss, (edge.shape[0], edge_rows.shape[2] - BANDS))
        edge_rows[j] = jnp.concatenate([edge - shift, spare], axis=1)
    even = product(jnp.concatenate(grads[0], axis=0), even_ref, NT, 1, 1)
    odd = product(jnp.concatenate(grads[1], axis=0), odd_ref, NT, 1, 1)
    even = even - jnp.concatenate(shifts, axis=0)
    held_ref[:, :half] = even + odd
    held_ref[:, half:] = even - odd
    for s in range(devices):
        other = lax.bitwise_xor(me, s)
        out_refs[s][:rows, :] = held_ref[:, pl.ds(pl.multiple_of(other * frames, frames), frames)]
        for j in range(per):
            out_refs[s][rows + j : rows + j + 1, :] = edge_rows[j, pl.ds(other, 1), :]


def synthesise(devices, per, far, me_ref, len_ref, stft_ref, newest_ref, ratio_ref, prev_ref, first_ref,
               *rest):
    count = devices // 2
    piece_refs, rest = rest[:count], rest[count:]
    win_ref, even_ref, odd_ref, filt_ref, even_back_ref, odd_back_ref = rest[:6]
    out_ref, loss_ref, carry, edges, *powers = rest[8 if far else 6 :]
    records, half = carry.shape
    quarter = half // 2
    frames = powers[0].shape[0] // records
    step, last = pl.program_id(0), pl.num_programs(0) - 1
    w0, w1 = win_ref[0:1, :half], win_ref[0:1, half:]

    def back(bins, grads):
        even, odd = (
            product(b * jnp.concatenate([g, g], axis=1), table, NN)
            for b, g, table in zip(bins, grads, (even_back_ref, odd_back_ref))
        )
        return (even + odd) * w0, (even - odd) * w1

    @pl.when(step == 0)
    def _():
        me = me_ref[0]
        lowest = (me // count ^ far) * records
        for s in range(count):
            for j in range(per):
                record = swapped(me, s + far * count, per, j) - lowest
                grad = ratio_ref[s, j] * piece_refs[s][j * BANDS : (j + 1) * BANDS, :]
                grad = product(grad, filt_ref, TN, 0, 0)
                for which, power in enumerate(powers):
                    power[pl.ds(record, frames, stride=records), :] = grad[
                        :, which * quarter : (which + 1) * quarter
                    ]
                row = per * BANDS + j
                edges[pl.ds(record, 1), :] = piece_refs[s][row : row + 1, :]
        bins = spectrum(prev_ref[...] * w0, first_ref[...] * w1, even_ref, odd_ref)
        power = jnp.concatenate([power_of(b) for b in bins], axis=1)
        base = product(power, filt_ref, NT, 1, 1) + 0.05
        row = lax.broadcasted_iota(jnp.int32, base.shape, 0)
        lens = jnp.zeros(base.shape, jnp.int32)
        for record in range(records):
            lens = jnp.where(row == record, len_ref[lowest + record], lens)
        at = me * frames - 1
        grad = jnp.where((at < lens) & (at >= 0), compress(base)[1] * edges[:, :BANDS], 0.0)
        grad = product(grad, filt_ref, NN)
        carry[...] = back(bins, (grad[:, :quarter], grad[:, quarter:]))[1]
        row = lax.broadcasted_iota(jnp.int32, edges.shape, 0) + lowest
        lane = lax.broadcasted_iota(jnp.int32, edges.shape, 1)
        losses = jnp.broadcast_to(edges[:, BANDS : BANDS + 1], edges.shape)
        losses = jnp.sum(jnp.where(row == lane, losses, 0.0), axis=0, keepdims=True)
        loss_ref[...] = losses + rest[7][...] if far else losses

    size = BACK_CHUNK * records
    rows = pl.ds(pl.multiple_of(step * size, size), size)
    bins = stft_ref[...].reshape(size, 2 * half)
    final = jnp.where(step == last, newest_ref[...], bins[size - records :])
    bins = jnp.concatenate([bins[: size - records], final], axis=0)
    leading, trailing = back((bins[:, :half], bins[:, half:]), [power[rows, :] for power in powers])
    before = carry[...]
    for t in range(BACK_CHUNK):
        out_ref[:, half * t : half * (t + 1)] = leading[records * t : records * (t + 1)] + before
        before = trailing[records * t : records * (t + 1)]
    carry[...] = before


def whole(shape):
    return pl.BlockSpec(shape, lambda i, *_: (0,) * len(shape))


def send_order(devices):
    near, far = list(range(1, devices // 2)), list(range(devices // 2, devices))
    return [s for pair in zip(far, near + [0]) for s in pair if s] + [0]


def exchange(values, devices):
    moved = list(values)
    for s in send_order(devices)[:-1]:
        moved[s] = lax.ppermute(values[s], "tm", [(i, i ^ s) for i in range(devices)])
    return moved


def in_hbm(array):
    return pltpu.with_memory_space_constraint(jnp.asarray(array), pltpu.HBM)


def shape_of(array):
    return jax.ShapeDtypeStruct(array.shape, array.dtype)


def fast_body(wave, target_mod, lengths):
    records, half = wave.shape[0], FFT // 2
    frames = wave.shape[1] // half
    devices = lax.axis_size("tm")
    rows, count = target_mod.shape
    per = rows // BANDS
    me = lax.axis_index("tm").astype(jnp.int32).reshape(1)
    steps = frames // CHUNK
    window = np.broadcast_to(host_window(FFT)[None], (8, FFT))
    even, odd = host_halves(FFT)
    filters = host_filters(half, BANDS)
    filters = np.concatenate([filters[0::2], filters[1::2]], axis=0).T
    length = frames * devices
    mod_even, mod_odd = host_modulation(length, count)
    edge_tables = []
    for table, sign in ((mod_even, 1.0), (mod_odd, -1.0)):
        both = np.concatenate([table, sign * table], axis=0)
        picked = [both[frames * d - 1][None] for d in range(devices)]
        edge_tables.append(paired(np.concatenate(picked + [np.zeros((-devices % 16, count))], axis=0)))
    edge_table = np.stack(edge_tables)
    even, odd, filters, mod_even, mod_odd = (paired(t) for t in (even, odd, filters, mod_even, mod_odd))
    tables = [in_hbm(t) for t in (window, even, odd, filters)]
    back_tables = tables + [in_hbm(t.swapaxes(1, 2)) for t in (even, odd)]
    wave_here = in_hbm(wave)
    smem = pl.BlockSpec(memory_space=pltpu.SMEM)
    params = pltpu.CompilerParams(vmem_limit_bytes=48 * 2**20)
    order = send_order(devices)

    halo = from_behind(wave[:, :half], "tm", -1)
    stft, env, ratio = pl.pallas_call(
        functools.partial(analyse, devices, per),
        name="analyse",
        grid=(steps,),
        in_specs=[
            smem,
            smem,
            pl.BlockSpec((records, CHUNK * half), lambda i: (0, i)),
            pl.BlockSpec((records, half), lambda i: (0, jnp.minimum((i + 1) * CHUNK, frames - 1))),
        ]
        + [whole(t.shape) for t in tables],
        out_specs=[pl.BlockSpec((CHUNK, records, FFT), lambda i: (i, 0, 0))]
        + [whole((devices, per, BANDS, frames))] * 2,
        out_shape=[jax.ShapeDtypeStruct((frames, records, FFT), F32)]
        + [jax.ShapeDtypeStruct((devices, per, BANDS, frames), F32)] * 2,
        scratch_shapes=[pltpu.VMEM((frames * records, half // 2), F32)] * 2,
        compiler_params=params,
    )(me, lengths, wave_here, wave_here, *tables)

    def finish_in_order(*refs):
        inputs, outs, power = refs[:13], refs[13 : 13 + devices], refs[-1]
        finish(devices, per, *inputs, *[outs[order.index(s)] for s in range(devices)], power)

    newest, ratio, last_block, *envs = pl.pallas_call(
        finish_in_order,
        name="finish",
        grid=(1,),
        in_specs=[smem, smem, pl.BlockSpec((records, half), lambda i: (0, frames - 1)), whole(halo.shape)]
        + [whole(t.shape) for t in tables]
        + [whole(env.shape)] * 2,
        out_specs=[whole((records, FFT)), whole(ratio.shape), whole(halo.shape)]
        + [whole((rows, frames))] * devices,
        out_shape=[jax.ShapeDtypeStruct((records, FFT), F32), shape_of(ratio), shape_of(halo)]
        + [jax.ShapeDtypeStruct((rows, frames), F32)] * devices,
        scratch_shapes=[pltpu.VMEM((records, half), F32)],
        compiler_params=params,
    )(me, lengths, wave_here, halo, *tables, env, ratio)

    envs = exchange([envs[order.index(s)] for s in range(devices)], devices)
    prev = from_behind(last_block, "tm", 1)
    padded = rows + 8
    bin_order = host_order(count)

    def modulate_in_order(me_ref, len_ref, _, *refs):
        ins, rest = refs[:devices], refs[devices:]
        outs = rest[5 : 5 + devices]
        modulate(devices, per, me_ref, len_ref, *[ins[order.index(s)] for s in range(devices)], *rest[:5],
                 *[outs[order.index(s)] for s in range(devices)], *rest[5 + devices :])

    grads = pl.pallas_call(
        modulate_in_order,
        name="modulate",
        grid=(1,),
        in_specs=[smem, smem, pl.BlockSpec(memory_space=pl.ANY)]
        + [whole((rows, frames))] * devices
        + [whole(a.shape) for a in (target_mod, bin_order, mod_even, mod_odd, edge_table)],
        out_specs=[whole((padded, frames))] * devices,
        out_shape=[jax.ShapeDtypeStruct((padded, frames), F32)] * devices,
        scratch_shapes=[
            pltpu.VMEM((rows, length), F32),
            pltpu.VMEM((per, edge_table.shape[2], frames), F32),
        ],
        compiler_params=params,
    )(me, lengths, prev, *[envs[s] for s in order], target_mod, bin_order, mod_even, mod_odd, edge_table)
    grads = exchange([grads[order.index(s)] for s in range(devices)], devices)

    side, tall = devices // 2, records // 2
    grad_wave, loss = (), ()
    for far in range(2):
        def tile(ref, far=far):
            return ref[0] // side ^ far

        grad_wave, loss = pl.pallas_call(
            functools.partial(synthesise, devices, per, far),
            name="synthesise",
            grid_spec=pltpu.PrefetchScalarGridSpec(
                num_scalar_prefetch=1,
                grid=(frames // BACK_CHUNK,),
                in_specs=[
                    smem,
                    pl.BlockSpec((BACK_CHUNK, tall, FFT), lambda i, ref, tile=tile: (i, tile(ref), 0)),
                    pl.BlockSpec((tall, FFT), lambda i, ref, tile=tile: (tile(ref), 0)),
                    pl.BlockSpec((side, per, BANDS, frames), lambda i, ref, far=far: (far, 0, 0, 0)),
                    pl.BlockSpec((tall, half), lambda i, ref, tile=tile: (tile(ref), 0)),
                    pl.BlockSpec((tall, half), lambda i, ref, tile=tile: (tile(ref), 0)),
                ]
                + [whole((padded, frames))] * side
                + [whole(t.shape) for t in back_tables]
                + [pl.BlockSpec(memory_space=pl.ANY), whole((1, frames))][: 2 * far],
                out_specs=[
                    pl.BlockSpec((tall, BACK_CHUNK * half), lambda i, ref, tile=tile: (tile(ref), i)),
                    whole((1, frames)),
                ],
                scratch_shapes=[pltpu.VMEM((tall, half), F32), pltpu.VMEM((tall, frames), F32)]
                + [pltpu.VMEM((frames * tall, half // 2), F32)] * 2,
            ),
            out_shape=[shape_of(wave), jax.ShapeDtypeStruct((1, frames), F32)],
            input_output_aliases={13 + side: 0} if far else {},
            compiler_params=params,
        )(me, lengths, stft, newest, ratio, prev, wave_here, *grads[far * side : (far + 1) * side], *back_tables,
          *((grad_wave, loss) if far else ()))
    return grad_wave, loss[0, :records]


def body(wave, target_mod, lengths):
    devices = lax.axis_size("tm")
    frames = wave.shape[1] // (FFT // 2)
    rows, count = target_mod.shape
    whole_records = rows % BANDS == 0 and rows * devices == wave.shape[0] * BANDS
    if whole_records and devices & (devices - 1) == 0 and frames == 128 and count % 256 == 0 and wave.shape[0] == 16:
        return fast_body(wave, target_mod, lengths)
    return general_body(wave, target_mod, lengths)


def solution(mesh):
    in_specs = (P("rec", "tm"), P(("rec", "tm"), None), P("rec"))
    out_specs = (P("rec", "tm"), P("rec"))
    return jax.shard_map(body, mesh=mesh, in_specs=in_specs, out_specs=out_specs, check_vma=False)
```

```python
import functools
import math

import jax
import jax.numpy as jnp
import numpy as np
from jax import lax
from jax.experimental import pallas as pl
from jax.experimental.pallas import tpu as pltpu
from jax.sharding import PartitionSpec as P

FFT = 512
BANDS = 96


HIGH = lax.Precision.HIGHEST
rate_hz = 16000.0


def from_behind(array, axis, by):
    count = lax.axis_size(axis)
    pairs = [(i, i + by) for i in range(count) if 0 <= i + by < count]
    return lax.ppermute(array, axis, pairs)


def a_weight(freq):
    square = freq * freq
    upper = 12194.0**2 * square * square
    lower = (
        (square + 20.6**2)
        * jnp.sqrt((square + 107.7**2) * (square + 737.9**2))
        * (square + 12194.0**2)
    )
    return upper / lower


def bark_scale(freq):
    return 13.0 * jnp.arctan(0.00076 * freq) + 3.5 * jnp.arctan((freq / 7500.0) ** 2)


def band_table(bins, bands):
    freq = jnp.arange(bins, dtype=jnp.float32) * (rate_hz / (2.0 * bins))
    height = bark_scale(freq)
    top_bark = bark_scale(jnp.asarray(rate_hz / 2.0, jnp.float32))
    centres = (jnp.arange(bands, dtype=jnp.float32) + 0.5) * (top_bark / bands)
    spread = jnp.maximum(0.5, 2.0 * top_bark / bands)
    shape = jnp.maximum(0.0, 1.0 - jnp.abs(height[:, None] - centres[None, :]) / spread)
    weight = 0.1 + a_weight(freq) / a_weight(jnp.asarray(1000.0, jnp.float32))
    return shape * weight[:, None] / jnp.maximum(jnp.sum(shape, axis=0), 1.0)[None, :]


def spectral_table(size):
    bins = size // 2
    index = (
        jnp.arange(size, dtype=jnp.int32)[:, None]
        * jnp.arange(bins, dtype=jnp.int32)[None, :]
        % size
    )
    angle = index.astype(jnp.float32) * (2.0 * math.pi / size)
    return jnp.concatenate([jnp.cos(angle), -jnp.sin(angle)], axis=1) * (1.0 / math.sqrt(size))


def hann_window(size):
    return 0.5 - 0.5 * jnp.cos(jnp.arange(size, dtype=jnp.float32) * (2.0 * math.pi / size))


def modulation_table(times, count, length):
    index = times[:, None] * jnp.arange(1, count + 1, dtype=jnp.int32)[None, :] % length
    angle = index.astype(jnp.float32) * (2.0 * math.pi / length)
    return jnp.concatenate([jnp.cos(angle), -jnp.sin(angle)], axis=1) * (1.0 / math.sqrt(length))


def general_body(wave, target_mod, lengths):
    records = wave.shape[0]
    half = FFT // 2
    frames_dev = wave.shape[1] // half
    devices = lax.axis_size("tm")
    position = lax.axis_index("tm")
    rows_dev = target_mod.shape[0]
    count = target_mod.shape[1]
    frames_all = frames_dev * devices
    window = hann_window(FFT)
    spectral = spectral_table(FFT)
    filters = band_table(half, BANDS)
    blocks = wave.reshape(records, frames_dev, half)
    following = from_behind(blocks[:, 0, :], "tm", -1)
    extended = jnp.concatenate([blocks, following[:, None, :]], axis=1)
    frames = jnp.concatenate([extended[:, :-1], extended[:, 1:]], axis=2) * window
    spectrum = jnp.einsum("rfn,nk->rfk", frames, spectral, precision=HIGH)
    real_stft = spectrum[..., :half]
    imag_stft = spectrum[..., half:]
    power = real_stft * real_stft + imag_stft * imag_stft
    energy = jnp.einsum("rfk,kb->rbf", power, filters, precision=HIGH)
    envelope = (energy + 0.05) ** 0.3
    times = position * frames_dev + jnp.arange(frames_dev, dtype=jnp.int32)
    valid = (times[None, :] < lengths[:, None]).astype(jnp.float32)
    masked = envelope * valid[:, None, :]
    counts = lengths.astype(jnp.float32) * BANDS
    partial_value = jnp.sum(masked, axis=(1, 2))
    row_ids = position * rows_dev + jnp.arange(rows_dev, dtype=jnp.int32)
    owner = row_ids // BANDS
    picker = (owner[:, None] == jnp.arange(records, dtype=jnp.int32)[None, :]).astype(jnp.float32)
    flat = masked.reshape(records * BANDS, frames_dev)
    full_table = modulation_table(jnp.arange(frames_all, dtype=jnp.int32), count, frames_all)
    stacked = flat.reshape(devices, rows_dev, frames_dev)
    spectra = jnp.dot(
        lax.all_to_all(stacked, "tm", split_axis=0, concat_axis=2, tiled=True)[0],
        full_table,
        precision=HIGH,
        preferred_element_type=jnp.float32,
    )
    loudness = lax.psum(partial_value, "tm") / counts + 1e-05
    spectra = spectra / jnp.dot(picker, loudness, precision=HIGH)[:, None]
    real_mod = spectra[:, :count]
    imag_mod = spectra[:, count:]
    mod_power = real_mod * real_mod + imag_mod * imag_mod
    mismatch = jnp.log1p(mod_power) - target_mod
    factor = 2.0 * mismatch / (1.0 + mod_power)
    grad_real = factor * real_mod
    grad_imag = factor * imag_mod
    loss_part = jnp.dot(0.5 * jnp.sum(mismatch * mismatch, axis=1), picker, precision=HIGH)
    inner_part = jnp.dot(
        jnp.sum(grad_real * real_mod + grad_imag * imag_mod, axis=1), picker, precision=HIGH
    )
    loss, inner = lax.psum((loss_part, inner_part), "tm")
    grad_spectra = jnp.concatenate([grad_real, grad_imag], axis=1)
    grad_bands = lax.dot_general(
        grad_spectra,
        full_table,
        (((1,), (1,)), ((), ())),
        precision=HIGH,
        preferred_element_type=jnp.float32,
    )
    grad_rows = lax.all_to_all(grad_bands, "tm", split_axis=1, concat_axis=0, tiled=True)
    grad_normed = grad_rows.reshape(records, BANDS, frames_dev)
    grad_env = (
        (grad_normed - (inner / counts)[:, None, None])
        / loudness[:, None, None]
        * valid[:, None, :]
    )
    grad_energy = 0.3 * (energy + 0.05) ** (-0.7) * grad_env
    grad_power = jnp.einsum("rbf,kb->rfk", grad_energy, filters, precision=HIGH)
    grad_spectrum = jnp.concatenate(
        [2.0 * real_stft * grad_power, 2.0 * imag_stft * grad_power], axis=2
    )
    grad_frames = jnp.einsum("rfk,nk->rfn", grad_spectrum, spectral, precision=HIGH) * window
    leading = grad_frames[..., :half]
    trailing = grad_frames[..., half:]
    arrived = from_behind(trailing[:, -1, :], "tm", 1)
    moved = jnp.concatenate([arrived[:, None, :], trailing[:, :-1]], axis=1)
    grad_wave = (leading + moved).reshape(records, frames_dev * half)
    return (grad_wave, loss)


F32, BF16 = jnp.float32, jnp.bfloat16
CHUNK, BACK_CHUNK = 64, 64


def split_table(table):
    table = np.asarray(table, np.float32)
    high = table.astype(BF16)
    low = (table - high.astype(np.float32)).astype(BF16)
    return high, low


def paired(table):
    return np.stack(split_table(table))


def host_window(size):
    return (0.5 - 0.5 * np.cos(np.arange(size) * (2.0 * np.pi / size))).astype(np.float32)


def host_filters(bins, bands):
    freq = np.arange(bins) * (rate_hz / (2.0 * bins))

    def bark(f):
        return 13.0 * np.arctan(0.00076 * f) + 3.5 * np.arctan((f / 7500.0) ** 2)

    def weight_of(f):
        square = f * f
        upper = 12194.0**2 * square * square
        lower = (
            (square + 20.6**2)
            * np.sqrt((square + 107.7**2) * (square + 737.9**2))
            * (square + 12194.0**2)
        )
        return upper / lower

    height, top = bark(freq), bark(rate_hz / 2.0)
    centres = (np.arange(bands) + 0.5) * (top / bands)
    spread = max(0.5, 2.0 * top / bands)
    shape = np.maximum(0.0, 1.0 - np.abs(height[:, None] - centres[None, :]) / spread)
    weight = 0.1 + weight_of(freq) / weight_of(1000.0)
    return shape * weight[:, None] / np.maximum(shape.sum(axis=0), 1.0)[None, :]


def host_halves(size):
    half, quarter = size // 2, size // 4
    n, m = np.arange(half)[:, None], np.arange(quarter)[None, :]
    tables = []
    for odd in range(2):
        angle = (n * (2 * m + odd) % size) * (2.0 * np.pi / size)
        tables.append(np.concatenate([np.cos(angle), -np.sin(angle)], axis=1) / np.sqrt(size))
    return tables


def host_modulation(length, count):
    tables = []
    for first in (2, 1):
        index = np.arange(length // 2)[:, None] * np.arange(first, count + 1, 2)[None, :] % length
        angle = index * (2.0 * np.pi / length)
        tables.append(np.concatenate([np.cos(angle), -np.sin(angle)], axis=1) / np.sqrt(length))
    return tables


def host_order(count):
    order = np.concatenate([np.arange(1, count, 2), np.arange(0, count, 2)])
    return (np.arange(count)[:, None] == order[None, :]).astype(BF16)


def parts(value):
    high = value.astype(BF16)
    return high, (value - high.astype(F32)).astype(BF16)


NN, NT, TN = (((1,), (0,)), ((), ())), (((1,), (1,)), ((), ())), (((0,), (0,)), ((), ()))


def product(value, table, dims, axis=1, table_axis=0):
    high, low = parts(value)
    left = jnp.concatenate([high, low, high], axis=axis)
    right = jnp.concatenate([table[0], table[0], table[1]], axis=table_axis)
    return lax.dot_general(left, right, dims, preferred_element_type=F32)


def swapped(position, s, per, j):
    return lax.bitwise_xor(position, s) * per + j


def spectrum(left, right, even, odd):
    return product(left + right, even, NN), product(left - right, odd, NN)


def power_of(bins):
    quarter = bins.shape[1] // 2
    return bins[:, :quarter] * bins[:, :quarter] + bins[:, quarter:] * bins[:, quarter:]


def band_energy(power, filters):
    high, low = parts(power)
    right = jnp.concatenate([high, low, high], axis=1)
    left = jnp.concatenate([filters[0], filters[0], filters[1]], axis=1)
    return lax.dot_general(left, right, NT, preferred_element_type=F32) + 0.05


def compress(base):
    envelope = jnp.exp(0.3 * jnp.log(base))
    return envelope, 0.6 * envelope / base


def analyse(devices, per, far, me_ref, len_ref, x_ref, next_ref, win_ref, even_ref, odd_ref, filt_ref,
            *rest):
    stft_ref, env_ref, ratio_ref, *powers = rest[len(rest) - 5 :]
    records, half = next_ref.shape
    frames = powers[0].shape[0] // records
    step, last = pl.program_id(0), pl.num_programs(0) - 1
    w0, w1 = win_ref[0:1], win_ref[1:2]
    left, right = [], []
    for t in range(CHUNK):
        left.append(x_ref[:, half * t : half * (t + 1)] * w0)
        after = x_ref[:, half * (t + 1) : half * (t + 2)] if t + 1 < CHUNK else next_ref[...]
        right.append(after * w1)
    size = CHUNK * records
    rows = pl.ds(pl.multiple_of(step * size, size), size)
    left, right = jnp.concatenate(left, axis=0), jnp.concatenate(right, axis=0)
    for which, bins in enumerate(spectrum(left, right, even_ref, odd_ref)):
        stft_ref[:, :, which * half : (which + 1) * half] = bins.reshape(CHUNK, records, half)
        powers[which][rows, :] = power_of(bins)

    @pl.when(step == last)
    def _():
        me = me_ref[0]
        side = devices // 2
        lowest = (me // side ^ far) * records
        times = me * frames + lax.broadcasted_iota(jnp.int32, (BANDS, frames), 1)
        for s in range(side):
            for j in range(per):
                record = swapped(me, s + far * side, per, j)
                at = pl.ds(record - lowest, frames, stride=records)
                mine = jnp.concatenate([power[at, :] for power in powers], axis=1)
                envelope, ratio = compress(band_energy(mine, filt_ref))
                valid = times < len_ref[record]
                env_ref[s, j] = jnp.where(valid, envelope, 0.0)
                ratio_ref[s, j] = jnp.where(valid, ratio, 0.0)


def finish(devices, per, far, me_ref, len_ref, last_ref, halo_ref, win_ref, even_ref, odd_ref, filt_ref,
           env_ref, ratio_ref, stft_ref, out_ratio_ref, *rest):
    side = devices // 2
    out_refs, power = rest[:side], rest[side]
    records, _ = halo_ref.shape
    frames = env_ref.shape[3]
    me = me_ref[0]
    lowest = (me // side ^ far) * records
    w0, w1 = win_ref[0:1], win_ref[1:2]
    bins = spectrum(last_ref[...] * w0, halo_ref[...] * w1, even_ref, odd_ref)
    stft_ref[...] = jnp.concatenate(bins, axis=1)
    power[...] = jnp.concatenate([power_of(b) for b in bins], axis=1)
    places = [swapped(me, s + far * side, per, j) for s in range(side) for j in range(per)]
    ordered = [power[pl.ds(place - lowest, 1), :] for place in places]
    envelope, ratio = compress(band_energy(jnp.concatenate(ordered, axis=0), filt_ref))
    newest = lax.broadcasted_iota(jnp.int32, (BANDS, frames), 1) == frames - 1
    at = me * frames + frames - 1
    for s in range(side):
        for j in range(per):
            k = s * per + j
            valid = at < len_ref[places[k]]
            here = jnp.where(valid, envelope[:, k : k + 1], 0.0)
            out_refs[s][j * BANDS : (j + 1) * BANDS, :] = jnp.where(newest, here, env_ref[s, j])
            here = jnp.where(valid, ratio[:, k : k + 1], 0.0)
            out_ratio_ref[s, j] = jnp.where(newest, here, ratio_ref[s, j])


def modulate(devices, per, me_ref, len_ref, *rest):
    env_refs, rest = rest[:devices], rest[devices:]
    target_ref, order_ref, even_ref, odd_ref, edge_ref = rest[:5]
    out_refs, (held_ref, edge_rows) = rest[5 : 5 + devices], rest[5 + devices :]
    me = me_ref[0]
    rows, frames = env_refs[0].shape
    count = target_ref.shape[1]
    middle = count // 2
    half = held_ref.shape[1] // 2
    for s in range(devices):
        at = pl.ds(pl.multiple_of(lax.bitwise_xor(me, s) * frames, frames), frames)
        held_ref[:, at] = env_refs[s][...]
    early, late = held_ref[:, :half], held_ref[:, half:]
    total = early + late
    spectra = product(total, even_ref, NN), product(early - late, odd_ref, NN)
    target = target_ref[...]
    high, low = parts(target)
    least = (target - high.astype(F32) - low.astype(F32)).astype(BF16)
    order = order_ref[...]
    target = lax.dot_general(
        jnp.concatenate([high, low, least], axis=1),
        jnp.concatenate([order, order, order], axis=0),
        NN,
        preferred_element_type=F32,
    )
    grads, shifts = [[], []], []
    for j in range(per):
        at = slice(j * BANDS, (j + 1) * BANDS)
        counts = len_ref[me * per + j].astype(F32) * BANDS
        loudness = jnp.sum(total[at], axis=(0, 1), keepdims=True) / counts + 1e-05
        loss, inner = jnp.zeros((1, 1), F32), jnp.zeros((1, 1), F32)
        for which in range(2):
            mine = spectra[which][at] / loudness
            real, imag = mine[:, :middle], mine[:, middle:]
            mod_power = real * real + imag * imag
            mismatch = jnp.log1p(mod_power) - target[at, which * middle : (which + 1) * middle]
            factor = 2.0 * mismatch / (1.0 + mod_power)
            loss += 0.5 * jnp.sum(mismatch * mismatch, axis=(0, 1), keepdims=True)
            inner += jnp.sum(factor * mod_power, axis=(0, 1), keepdims=True)
            factor = factor / loudness
            grads[which].append(jnp.concatenate([factor * real, factor * imag], axis=1))
        shift = inner / counts / loudness
        shifts.append(jnp.broadcast_to(shift, (BANDS, 1)))
        edge = jnp.zeros((edge_ref.shape[2], BANDS), F32)
        for which in range(2):
            high, low = parts(grads[which][j])
            left = jnp.concatenate([edge_ref[which, 0], edge_ref[which, 0], edge_ref[which, 1]], axis=1)
            right = jnp.concatenate([high, low, high], axis=1)
            edge += lax.dot_general(left, right, NT, preferred_element_type=F32)
        spare = jnp.broadcast_to(loss, (edge.shape[0], edge_rows.shape[2] - BANDS))
        edge_rows[j] = jnp.concatenate([edge - shift, spare], axis=1)
    even = product(jnp.concatenate(grads[0], axis=0), even_ref, NT, 1, 1)
    odd = product(jnp.concatenate(grads[1], axis=0), odd_ref, NT, 1, 1)
    even = even - jnp.concatenate(shifts, axis=0)
    held_ref[:, :half] = even + odd
    held_ref[:, half:] = even - odd
    for s in range(devices):
        other = lax.bitwise_xor(me, s)
        out_refs[s][:rows, :] = held_ref[:, pl.ds(pl.multiple_of(other * frames, frames), frames)]
        for j in range(per):
            out_refs[s][rows + j : rows + j + 1, :] = edge_rows[j, pl.ds(other, 1), :]


def synthesise(devices, per, far, me_ref, len_ref, stft_ref, newest_ref, ratio_ref, prev_ref, first_ref,
               *rest):
    count = devices // 2
    piece_refs, rest = rest[:count], rest[count:]
    win_ref, even_ref, odd_ref, filt_ref, even_back_ref, odd_back_ref = rest[:6]
    out_ref, loss_ref, carry, edges, *powers = rest[8 if far else 6 :]
    records, half = carry.shape
    quarter = half // 2
    frames = powers[0].shape[0] // records
    step, last = pl.program_id(0), pl.num_programs(0) - 1
    w0, w1 = win_ref[0:1], win_ref[1:2]

    def back(bins, grads):
        even, odd = (
            product(b * jnp.concatenate([g, g], axis=1), table, NN)
            for b, g, table in zip(bins, grads, (even_back_ref, odd_back_ref))
        )
        return (even + odd) * w0, (even - odd) * w1

    @pl.when(step == 0)
    def _():
        me = me_ref[0]
        lowest = (me // count ^ far) * records
        for s in range(count):
            for j in range(per):
                record = swapped(me, s + far * count, per, j) - lowest
                grad = ratio_ref[s, j] * piece_refs[s][j * BANDS : (j + 1) * BANDS, :]
                grad = product(grad, filt_ref, TN, 0, 0)
                for which, power in enumerate(powers):
                    power[pl.ds(record, frames, stride=records), :] = grad[
                        :, which * quarter : (which + 1) * quarter
                    ]
                row = per * BANDS + j
                edges[pl.ds(record, 1), :] = piece_refs[s][row : row + 1, :]
        bins = spectrum(prev_ref[...] * w0, first_ref[...] * w1, even_ref, odd_ref)
        power = jnp.concatenate([power_of(b) for b in bins], axis=1)
        base = product(power, filt_ref, NT, 1, 1) + 0.05
        row = lax.broadcasted_iota(jnp.int32, base.shape, 0)
        lens = jnp.zeros(base.shape, jnp.int32)
        for record in range(records):
            lens = jnp.where(row == record, len_ref[lowest + record], lens)
        at = me * frames - 1
        grad = jnp.where((at < lens) & (at >= 0), compress(base)[1] * edges[:, :BANDS], 0.0)
        grad = product(grad, filt_ref, NN)
        carry[...] = back(bins, (grad[:, :quarter], grad[:, quarter:]))[1]
        row = lax.broadcasted_iota(jnp.int32, edges.shape, 0) + lowest
        lane = lax.broadcasted_iota(jnp.int32, edges.shape, 1)
        losses = jnp.broadcast_to(edges[:, BANDS : BANDS + 1], edges.shape)
        losses = jnp.sum(jnp.where(row == lane, losses, 0.0), axis=0, keepdims=True)
        loss_ref[...] = (losses + rest[7][...])[0, : loss_ref.shape[0]] if far else losses

    size = BACK_CHUNK * records
    rows = pl.ds(pl.multiple_of(step * size, size), size)
    bins = stft_ref[...].reshape(size, 2 * half)
    final = jnp.where(step == last, newest_ref[...], bins[size - records :])
    bins = jnp.concatenate([bins[: size - records], final], axis=0)
    leading, trailing = back((bins[:, :half], bins[:, half:]), [power[rows, :] for power in powers])
    before = carry[...]
    for t in range(BACK_CHUNK):
        out_ref[:, half * t : half * (t + 1)] = leading[records * t : records * (t + 1)] + before
        before = trailing[records * t : records * (t + 1)]
    carry[...] = before


def whole(shape):
    return pl.BlockSpec(shape, lambda i, *_: (0,) * len(shape))


def send_order(devices):
    near, far = list(range(1, devices // 2)), list(range(devices // 2, devices))
    return [s for pair in zip(far, near + [0]) for s in pair if s] + [0]


def send(value, s, devices):
    return lax.ppermute(value, "tm", [(i, i ^ s) for i in range(devices)])


def in_hbm(array):
    return pltpu.with_memory_space_constraint(jnp.asarray(array), pltpu.HBM)


def fast_body(wave, target_mod, lengths):
    records, half = wave.shape[0], FFT // 2
    frames = wave.shape[1] // half
    devices = lax.axis_size("tm")
    rows, count = target_mod.shape
    per, side, tall = rows // BANDS, devices // 2, records // 2
    me = lax.axis_index("tm").astype(jnp.int32).reshape(1)
    window = host_window(FFT).reshape(2, half)
    even, odd = host_halves(FFT)
    filters = host_filters(half, BANDS)
    filters = np.concatenate([filters[0::2], filters[1::2]], axis=0).T
    length = frames * devices
    mod_even, mod_odd = host_modulation(length, count)
    edge_tables = []
    for table, sign in ((mod_even, 1.0), (mod_odd, -1.0)):
        both = np.concatenate([table, sign * table], axis=0)
        picked = [both[frames * d - 1][None] for d in range(devices)]
        edge_tables.append(paired(np.concatenate(picked + [np.zeros((-devices % 16, count))], axis=0)))
    edge_table = np.stack(edge_tables)
    even, odd, filters, mod_even, mod_odd = (paired(t) for t in (even, odd, filters, mod_even, mod_odd))
    tables = [window, even, odd, filters]
    back_tables = tables + [even.swapaxes(1, 2), odd.swapaxes(1, 2)]
    held = [in_hbm(t) for t in tables]
    wave_here, lengths = in_hbm(wave), in_hbm(lengths)
    smem, anywhere = pl.BlockSpec(memory_space=pltpu.SMEM), pl.BlockSpec(memory_space=pl.ANY)
    params = pltpu.CompilerParams(vmem_limit_bytes=48 * 2**20)

    def call(kernel, far, grid, ins, outs, scratch, args, aliases=None):
        def spec(entry):
            if not isinstance(entry, tuple):
                return entry
            if len(entry) == 1:
                return whole(entry[0])
            return pl.BlockSpec(entry[0], lambda i, ref: entry[1](i, ref[0] // side ^ far))

        return pl.pallas_call(
            kernel,
            grid_spec=pltpu.PrefetchScalarGridSpec(
                num_scalar_prefetch=1,
                grid=(grid,),
                in_specs=[smem] + [spec(e) for e in ins],
                out_specs=[spec(e) for e, _ in outs],
                scratch_shapes=[pltpu.VMEM(shape, F32) for shape in scratch],
            ),
            out_shape=[jax.ShapeDtypeStruct(shape, F32) for _, shape in outs],
            input_output_aliases=aliases or {},
            compiler_params=params,
        )(me, lengths, *args)

    banded = (side, per, BANDS, frames)
    powers = [(frames * tall, half // 2)] * 2

    def analysed(far, tables, after):
        return call(
            functools.partial(analyse, devices, per, far), far, frames // CHUNK,
            [
                ((tall, CHUNK * half), lambda i, tile: (tile, i)),
                ((tall, half), lambda i, tile: (tile, jnp.minimum((i + 1) * CHUNK, frames - 1))),
            ]
            + [(t.shape,) for t in tables] + [anywhere] * len(after),
            [
                (((CHUNK, tall, FFT), lambda i, tile: (i, 0, 0)), (frames, tall, FFT)),
                ((banded,), banded),
                ((banded,), banded),
            ],
            powers,
            [wave_here, wave_here, *tables, *after],
        )

    def finished(far, env, ratio):
        return call(
            functools.partial(finish, devices, per, far), far, 1,
            [
                ((tall, half), lambda i, tile: (tile, frames - 1)),
                ((tall, half), lambda i, tile: (tile, 0)),
            ]
            + [(t.shape,) for t in tables] + [(banded,)] * 2,
            [(((tall, FFT),), (tall, FFT)), ((banded,), banded)] + [(((rows, frames),), (rows, frames))] * side,
            [(tall, half)],
            [wave_here, halo, *tables, env, ratio],
        )

    stfts, newest, ratios = [None] * 2, [None] * 2, [None] * 2
    pieces = [None] * devices
    stfts[1], *rest = analysed(1, held, [])
    halo = from_behind(wave[:, :half], "tm", -1)
    newest[1], ratios[1], *pieces[side:] = finished(1, *rest)
    stfts[0], *rest = analysed(0, tables, [newest[1]])
    newest[0], ratios[0], *pieces[:side] = finished(0, *rest)
    arrived = list(pieces)
    for s in range(1, devices):
        arrived[s] = send(pieces[s], s, devices)
    prev = from_behind(wave[:, -half:], "tm", 1)

    order = send_order(devices)
    padded = rows + 8
    bin_order = host_order(count)

    def modulate_in_order(me_ref, len_ref, _, *refs):
        ins, rest = refs[:devices], refs[devices:]
        outs = rest[5 : 5 + devices]
        modulate(devices, per, me_ref, len_ref, *[ins[order.index(s)] for s in range(devices)], *rest[:5],
                 *[outs[order.index(s)] for s in range(devices)], *rest[5 + devices :])

    grads = call(
        modulate_in_order, 0, 1,
        [anywhere] + [((rows, frames),)] * devices
        + [(a.shape,) for a in (target_mod, bin_order, mod_even, mod_odd, edge_table)],
        [(((padded, frames),), (padded, frames))] * devices,
        [(rows, length), (per, edge_table.shape[2], frames)],
        [prev, *[arrived[s] for s in order], target_mod, bin_order, mod_even, mod_odd, edge_table],
    )
    grads = [grads[order.index(s)] for s in range(devices)]
    for s in range(1, devices):
        grads[s] = send(grads[s], s, devices)

    grad_wave, loss = (), ()
    for far in range(2):
        grad_wave, loss = call(
            functools.partial(synthesise, devices, per, far), far, frames // BACK_CHUNK,
            [
                ((BACK_CHUNK, tall, FFT), lambda i, tile: (i, 0, 0)),
                ((tall, FFT),),
                (banded,),
                ((tall, half), lambda i, tile: (tile, 0)),
                ((tall, half), lambda i, tile: (tile, 0)),
            ]
            + [((padded, frames),)] * side + [(t.shape,) for t in back_tables]
            + [anywhere, ((1, frames),)][: 2 * far],
            [
                (((tall, BACK_CHUNK * half), lambda i, tile: (tile, i)), wave.shape),
                (((records,),), (records,)) if far else (((1, frames),), (1, frames)),
            ],
            [(tall, half), (tall, frames)] + powers,
            [stfts[far], newest[far], ratios[far], prev, wave_here, *grads[far * side : (far + 1) * side],
             *back_tables] + ([grad_wave, loss] if far else []),
            {13 + side: 0} if far else {},
        )
    return grad_wave, loss


def fast_form(wave, rows, count, devices):
    records, frames = wave[0], wave[1] // (FFT // 2)
    shapes = rows % BANDS == 0 and rows * devices == records * BANDS and records == 16
    return shapes and devices & (devices - 1) == 0 and frames == 128 and count % 256 == 0


def body(wave, target_mod, lengths):
    if fast_form(wave.shape, *target_mod.shape, lax.axis_size("tm")):
        return fast_body(wave, target_mod, lengths)
    return general_body(wave, target_mod, lengths)


def solution(mesh):
    in_specs = (P("rec", "tm"), P(("rec", "tm"), None), P("rec"))
    out_specs = (P("rec", "tm"), P("rec"))
    step = jax.shard_map(body, mesh=mesh, in_specs=in_specs, out_specs=out_specs, check_vma=False)

    def whole_step(wave, target_mod, lengths):
        parts, devices = mesh.shape["rec"], mesh.shape["tm"]
        shape = wave.shape[0] // parts, wave.shape[1] // devices
        run = step
        if fast_form(shape, target_mod.shape[0] // (parts * devices), target_mod.shape[1], devices):
            run = step
        return run(wave, target_mod, lengths)

    return whole_step
```
